32 devices in a mesh: cuts: 8 (over z, core), row: 4 (over y, x).
Axes of the slice: x: 2, y: 2, z: 4, core: 2. Of those that a mesh axis runs over, the one named last changes fastest.
Arguments:
- field: float32 [2, 64, 256, 256], P(None, 'cuts', 'row'), may hold values from -6 to 6
- row_prop: float32 [2, 256, 256], replicated, may hold values from -0.25 to 0.25
- col_prop: float32 [2, 256, 256], replicated, may hold values from -0.25 to 0.25
- phase: float32 [64, 8192], P('cuts', 'row'), may hold values from -3.140625 to 3.140625
- energy: float32 [64, 8192], P('cuts', 'row'), may hold values from -6 to 6
- cells: int32 [64, 8192], P('cuts', 'row'), may hold values from 0 to 65535, as said below
- shifts: int32 [4], replicated, may hold values from 1 to 2, as said below
Outputs:
- field_out: float32 [2, 64, 256, 256], P(None, 'cuts', 'row')
- phase_out: float32 [64, 8192], P('cuts', 'row')
- energy_out: float32 [64, 8192], P('cuts', 'row')
- bunching: float32 [4, 2, 64], P(None, None, 'cuts')
The draws below stay inside these ranges and needn't reach their ends.
Inputs may be any that keep to these rules, and one draw needn't show every extreme that they name: `cells`: electron j of a slice sits in a grid row from b * 64 to (b + 1) * 64 - 1, where b = j // 2048. `shifts`: 2 slices slip in at least one period.
All inputs are finite; a program needn't handle non-finite values.
Results may differ from the reference program's by a relative error of at most 0.00021.
Values sent between devices are 32-bit elements; how exact they have to be, the bound alone decides.
No kernel may reach another device: no remote copies, remote signals or barrier semaphores. Data moves between devices by JAX's collectives and lax.ppermute only.
A program may use at most 64 MiB of HBM per device.

```python
import jax
import jax.numpy as jnp
from jax import lax

NR = 256
NC = 256
ELEC = 8192
PERIODS = 4
KMAX = 2
SLICES = 64
N_ROW = 4


def draw_cells(key, part):
    rows_dev = NR // N_ROW
    row_block = jnp.arange(ELEC, dtype=jnp.int32) // (ELEC // N_ROW)
    offset = jax.random.randint(jax.random.fold_in(key, 11), (SLICES, ELEC), 0, rows_dev * NC, dtype=jnp.int32)
    return (row_block[None, :] * (rows_dev * NC) + offset).astype(jnp.int32)


def draw_shifts(key, part):
    chosen = jax.random.randint(jax.random.fold_in(key, 21), (PERIODS,), 1, KMAX + 1, dtype=jnp.int32)
    marked = jax.random.randint(jax.random.fold_in(key, 22), (), 0, PERIODS, dtype=jnp.int32)
    return jnp.where(jnp.arange(PERIODS, dtype=jnp.int32) == marked, KMAX, chosen).astype(jnp.int32)


def steps_of(key, dims, cuts, low, top_value):
    loudness = 1.0
    for dim, parts in cuts:
        steps = jax.random.uniform(jax.random.fold_in(jax.random.fold_in(key, 6), dim), (parts,), jnp.float32, low / len(cuts), top_value / len(cuts))
        loudness = loudness * jnp.repeat(jnp.exp(steps), dims[dim] // parts).reshape((-1,) + (1,) * (len(dims) - 1 - dim))
    return loudness


def noise(stream_key, extent, spread, most, cuts=(), held_as=jnp.bfloat16):
    gain = steps_of(stream_key, extent, cuts, -0.22, 0.18) if cuts else 1.0
    array = jax.random.normal(stream_key, extent, jnp.float32) * spread * gain
    return jnp.minimum(jnp.maximum(array, -most), most).astype(held_as)


def setup_inputs(seed: int = 0) -> dict:
    splits = jax.random.split(jax.random.key(seed), 8)
    field = noise(splits[0], (2, SLICES, NR, NC), 1.0, 6.0, ((1, 8), (2, 4)), jnp.float32)
    row_prop = noise(splits[1], (2, NR, NR), (2 * NR) ** -0.5, 0.25, (), jnp.float32)
    col_prop = noise(splits[2], (2, NC, NC), (2 * NC) ** -0.5, 0.25, (), jnp.float32)
    phase = jnp.clip(jax.random.uniform(splits[3], (SLICES, ELEC), jnp.float32, -3.140625, 3.140625), -3.140625, 3.140625)
    energy = noise(splits[4], (SLICES, ELEC), 1.0, 6.0, ((0, 8), (1, 4)), jnp.float32)
    cells = draw_cells(jax.random.fold_in(splits[7], 71), 0)
    shifts = draw_shifts(jax.random.fold_in(splits[7], 71), 0)
    return {"field": field, "row_prop": row_prop, "col_prop": col_prop, "phase": phase, "energy": energy, "cells": cells, "shifts": shifts}


kick_rate = 0.5
source_gain = 0.5


def sweep_columns(prop, real_part, imag_part):
    def product(matrix, values):
        return jnp.einsum('ck,srk->src', matrix, values, precision=lax.Precision.HIGHEST)
    return (product(prop[0], real_part) - product(prop[1], imag_part),
            product(prop[0], imag_part) + product(prop[1], real_part))


def sweep_rows(prop, real_part, imag_part):
    def product(matrix, values):
        return jnp.einsum('rk,skc->src', matrix, values, precision=lax.Precision.HIGHEST)
    return (product(prop[0], real_part) - product(prop[1], imag_part),
            product(prop[0], imag_part) + product(prop[1], real_part))


def reference(field, row_prop, col_prop, phase, energy, cells, shifts):
    real_part = field[0]
    imag_part = field[1]
    count = real_part.shape[0]
    slice_index = jnp.arange(count, dtype=jnp.int32)[:, None]
    partials = []
    for period in range(PERIODS):
        start = (KMAX - shifts[period]).astype(jnp.int32)
        padding = jnp.zeros((KMAX, NR, NC), dtype=real_part.dtype)
        real_part = lax.dynamic_slice_in_dim(jnp.concatenate([padding, real_part], 0), start, count, 0)
        imag_part = lax.dynamic_slice_in_dim(jnp.concatenate([padding, imag_part], 0), start, count, 0)
        sample_real = jnp.take_along_axis(real_part.reshape(count, NR * NC), cells, axis=1)
        sample_imag = jnp.take_along_axis(imag_part.reshape(count, NR * NC), cells, axis=1)
        energy = energy - kick_rate * (sample_real * jnp.cos(phase) - sample_imag * jnp.sin(phase))
        phase = phase + energy
        emit_real = jnp.cos(phase)
        emit_imag = -jnp.sin(phase)
        partials.append(jnp.stack([jnp.sum(emit_real, 1), jnp.sum(emit_imag, 1)]))
        deposit_real = jnp.zeros((count, NR * NC), dtype=real_part.dtype).at[slice_index, cells].add(emit_real)
        deposit_imag = jnp.zeros((count, NR * NC), dtype=real_part.dtype).at[slice_index, cells].add(emit_imag)
        real_part = real_part + source_gain * deposit_real.reshape(count, NR, NC)
        imag_part = imag_part + source_gain * deposit_imag.reshape(count, NR, NC)
        real_part, imag_part = sweep_columns(col_prop, real_part, imag_part)
        real_part, imag_part = sweep_rows(row_prop, real_part, imag_part)
    bunching = jnp.stack(partials) * (ELEC ** -0.5)
    return jnp.stack([real_part, imag_part]), phase, energy, bunching
```

```python
import jax
import jax.numpy as jnp
from jax import lax
from jax.experimental import pallas as pl
from jax.experimental.pallas import tpu as pltpu
from jax.sharding import PartitionSpec as P

KMAX = 2
kick_rate = 0.5
source_gain = 0.5
BF = jnp.bfloat16
F32 = jnp.float32
LANES = 128
CHUNK = 512


def shifted(value, axis, steps):
    count = lax.axis_size(axis)
    initial, last = (max(0, -steps), min(count, count - steps))
    return lax.ppermute(value, axis, [(source, source + steps) for source in range(initial, last)])


def rows_product(matrix, values):
    return jnp.einsum("rk,skc->src", matrix, values, precision=lax.Precision.HIGHEST)


def cols_product(matrix, values):
    return jnp.einsum("ck,srk->src", matrix, values, precision=lax.Precision.HIGHEST)


def complex_rows(prop, values):
    return jnp.stack(
        [
            rows_product(prop[0], values[0]) - rows_product(prop[1], values[1]),
            rows_product(prop[0], values[1]) + rows_product(prop[1], values[0]),
        ]
    )


def row_blocks(field, row_prop, col_prop, phase, energy, cells, shifts):
    count = field.shape[1]
    row_count = field.shape[2]
    col_count = field.shape[3]
    row_start = lax.axis_index("row") * row_count
    local_cells = cells - row_start * col_count
    cell_row = local_cells // col_count
    cell_col = local_cells - cell_row * col_count
    row_pick = (
        cell_row[:, None, :] == jnp.arange(row_count, dtype=jnp.int32)[None, :, None]
    ).astype(jnp.float32)
    col_pick = (
        cell_col[:, :, None] == jnp.arange(col_count, dtype=jnp.int32)[None, None, :]
    ).astype(jnp.float32)
    own_prop = lax.dynamic_slice_in_dim(row_prop, row_start, row_count, 1)
    partials = []
    for period in range(shifts.shape[0]):
        last_slices = field[:, count - KMAX :]
        arrived = shifted(last_slices, "cuts", 1)
        joined = jnp.concatenate([arrived, field], axis=1)
        field = lax.dynamic_slice_in_dim(joined, KMAX - shifts[period], count, 1)
        by_column = jnp.einsum("psrc,sec->psre", field, col_pick, precision=lax.Precision.HIGHEST)
        samples = jnp.sum(by_column * row_pick[None], axis=2)
        sample_real = samples[0]
        sample_imag = samples[1]
        energy = energy - kick_rate * (sample_real * jnp.cos(phase) - sample_imag * jnp.sin(phase))
        phase = phase + energy
        emit_real = jnp.cos(phase)
        emit_imag = -jnp.sin(phase)
        local_sums = jnp.stack([jnp.sum(emit_real, 1), jnp.sum(emit_imag, 1)])
        partials.append(lax.psum(local_sums, "row"))
        emitted = jnp.stack([emit_real, emit_imag])
        weighted = row_pick[None] * emitted[:, :, None, :]
        deposit = jnp.einsum("psre,sec->psrc", weighted, col_pick, precision=lax.Precision.HIGHEST)
        field = field + source_gain * deposit
        field = jnp.stack(
            [
                cols_product(col_prop[0], field[0]) - cols_product(col_prop[1], field[1]),
                cols_product(col_prop[0], field[1]) + cols_product(col_prop[1], field[0]),
            ]
        )
        field = complex_rows(own_prop, lax.all_gather(field, "row", axis=2, tiled=True))
    bunching = jnp.stack(partials)
    bunching = bunching * (phase.shape[1] * lax.axis_size("row")) ** (-0.5)
    return (field, phase, energy, bunching)


def halves(value):
    high = value.astype(BF)
    return high, (value - high.astype(F32)).astype(BF)


def one_hot(index, size):
    shape = (size, index.shape[1])
    level = lax.broadcasted_iota(jnp.int32, shape, 0).astype(BF)
    return jnp.where(level == jnp.broadcast_to(index.astype(BF), shape), jnp.ones((), BF), jnp.zeros((), BF))


def chunks(length):
    step = CHUNK if length % CHUNK == 0 else length
    return [(start, step) for start in range(0, length, step)]


def vmem_call(kernel, outs, inputs, shifts=None, scratch=()):
    vmem = pl.BlockSpec(memory_space=pltpu.VMEM)
    specs = [vmem] * len(inputs)
    if shifts is not None:
        specs = [pl.BlockSpec(memory_space=pltpu.SMEM)] + specs
        inputs = [shifts] + list(inputs)
    return pl.pallas_call(
        kernel,
        out_shape=outs,
        in_specs=specs,
        out_specs=jax.tree.map(lambda _: vmem, outs),
        scratch_shapes=list(scratch),
        compiler_params=pltpu.CompilerParams(vmem_limit_bytes=48 * 1024 * 1024),
    )(*inputs)


def sds(shape, dtype=F32):
    return jax.ShapeDtypeStruct(shape, dtype)


def remainder(value, divisor):
    return lax.rem(value + 4 * divisor, jnp.int32(divisor))


class Plan:
    def __init__(self, n_cuts, n_row, field, phase, shifts):
        self.n_cuts, self.n_row = n_cuts, n_row
        self.per_cut, self.rows, self.cols = field.shape[1:]
        self.count = phase.shape[1]
        self.periods = shifts.shape[0]
        self.held = max(1, self.per_cut // n_row)
        self.slots = n_cuts * self.per_cut
        self.lines = self.held * n_row
        most, least = KMAX * self.periods, self.periods + 1
        self.lead = self.held * ((most - KMAX) // self.held)
        self.ahead = max(0, most - self.lead)
        self.behind = max(0, self.lead - least)
        self.turn = self.lead // self.held

    def fits(self):
        n = self.n_row
        if n & (n - 1) or self.per_cut % n or self.held < KMAX or self.count % LANES:
            return False
        return self.lead < self.per_cut and self.ahead <= self.held and self.behind <= self.held

    def send_pair(self, target):
        return (target - self.turn) % self.n_row, (self.turn + (target - self.turn) % self.n_row) // self.n_row

    def spread_table(self, d):
        table = []
        for c in range(self.n_cuts):
            for r in range(self.n_row):
                cuts_on = self.send_pair(r ^ d)[1]
                table.append((c * self.n_row + r, ((c + cuts_on) % self.n_cuts) * self.n_row + (r ^ d)))
        return table


def split_cells(cells, block, rows, cols):
    flat = cells.astype(jnp.int32)
    row = lax.div(flat, jnp.int32(cols))
    column = flat - row * cols
    return (row - block * rows).astype(F32), column.astype(F32)


def sample_line(values, row_ref, col_ref, real_ref, imag_ref, i, rows, cols, count):
    for start, step in chunks(count):
        here = (pl.ds(i, 1), pl.ds(start, step))
        found = jnp.dot(values, one_hot(col_ref[here], cols), preferred_element_type=F32)
        mask = lax.broadcasted_iota(jnp.int32, (rows, step), 0).astype(F32) == row_ref[here]
        real = jnp.where(mask, found[:rows] + found[rows : 2 * rows], 0.0)
        imag = jnp.where(mask, found[2 * rows : 3 * rows] + found[3 * rows :], 0.0)
        real_ref[here] = jnp.sum(real, 0, keepdims=True)
        imag_ref[here] = jnp.sum(imag, 0, keepdims=True)


def shifted_total(sc, period):
    total = sc[0]
    for step in range(1, period + 1):
        total = total + sc[step]
    return total


def kick(packet_ref, real_ref, imag_ref, fresh, period, count):
    real = jnp.where(fresh, 0.0, real_ref[...])
    imag = jnp.where(fresh, 0.0, imag_ref[...])
    phase = packet_ref[:, :count]
    energy = packet_ref[:, count : 2 * count]
    energy = energy - kick_rate * (real * jnp.cos(phase) - imag * jnp.sin(phase))
    phase = phase + energy
    emit_real = jnp.cos(phase)
    emit_imag = -jnp.sin(phase)
    packet_ref[:, :count] = phase
    packet_ref[:, count : 2 * count] = energy
    sums = packet_ref[:, 3 * count :]
    lane = lax.broadcasted_iota(jnp.int32, sums.shape, 1)
    sums = jnp.where(lane == 2 * period, jnp.sum(emit_real, 1, keepdims=True), sums)
    packet_ref[:, 3 * count :] = jnp.where(lane == 2 * period + 1, jnp.sum(emit_imag, 1, keepdims=True), sums)
    return emit_real, emit_imag


def first_kick(plan, field, phase, energy, cells, came, shifts):
    count, rows, cols, lines = plan.count, plan.rows, plan.cols, plan.per_cut

    def kernel(sc, field_ref, phase_ref, energy_ref, cells_ref, came_ref, *refs):
        outs = refs[: plan.n_row]
        packet_ref, row_ref, col_ref, real_ref, imag_ref = refs[plan.n_row :]
        me, cut = lax.axis_index("row"), lax.axis_index("cuts")
        parts = (phase_ref[...], energy_ref[...], cells_ref[...].astype(F32))
        for place, part in enumerate(parts):
            span = slice(place * count, (place + 1) * count)
            one = jnp.concatenate([part[1:], came_ref[:1, span]], 0)
            two = jnp.concatenate([part[2:], came_ref[:2, span]], 0)
            packet_ref[:, span] = jnp.where(sc[0] == 1, one, two)
        packet_ref[:, 3 * count :] = jnp.zeros((lines, LANES), F32)
        row_ref[...], col_ref[...] = split_cells(packet_ref[:, 2 * count : 3 * count], me, rows, cols)

        def line(i, carry):
            values = jnp.concatenate([*halves(field_ref[0, i]), *halves(field_ref[1, i])], 0)
            sample_line(values, row_ref, col_ref, real_ref, imag_ref, i, rows, cols, count)
            return carry

        lax.fori_loop(0, lines, line, 0)
        place = cut * plan.per_cut + lax.broadcasted_iota(jnp.int32, (lines, count), 0)
        kick(packet_ref, real_ref, imag_ref, remainder(place + sc[0], plan.slots) < sc[0], 0, count)
        for d in range(plan.n_row):
            pair = lax.rem((me ^ d) + plan.n_row * plan.turn - plan.turn, plan.n_row)
            for h in range(plan.held):
                outs[d][h : h + 1, :] = packet_ref[pl.ds(pair * plan.held + h, 1), :]

    width = 3 * count + LANES
    scratch = [pltpu.VMEM((lines, width), F32)] + [pltpu.VMEM((lines, count), F32)] * 4
    outs = [sds((plan.held, width))] * plan.n_row
    return vmem_call(kernel, outs, [field, phase, energy, cells, came], shifts, scratch)


def gather_packet(plan, pieces):
    count, lines = plan.count, plan.lines

    def kernel(*refs):
        packet_out, emit_out = refs[plan.n_row :]
        me = lax.axis_index("row")
        for d in range(plan.n_row):
            for h in range(plan.held):
                packet_out[pl.ds(h * plan.n_row + (me ^ d), 1), :] = refs[d][h : h + 1, :]
        phase = packet_out[:, :count]
        emit_out[:lines] = jnp.cos(phase)
        emit_out[lines:] = -jnp.sin(phase)

    return vmem_call(kernel, (sds((lines, 3 * count + LANES)), sds((2 * lines, count))), list(pieces))


def line_block(plan):
    return lax.rem(lax.broadcasted_iota(jnp.int32, (plan.lines, plan.count), 0), jnp.int32(plan.n_row))


def sample_and_kick(plan, period, grid, own, came, shifts):
    count, rows, cols, lines, n_row = plan.count, plan.rows, plan.cols, plan.lines, plan.n_row
    last = period + 1 == plan.periods
    width = 3 * count + LANES

    def kernel(sc, grid_ref, own_ref, came_ref, packet_out, emit_out, *refs):
        row_ref, col_ref, real_ref, imag_ref = refs[-4:]
        me, cut = lax.axis_index("row"), lax.axis_index("cuts")
        one = jnp.concatenate([own_ref[n_row:], came_ref[:n_row]], 0)
        two = came_ref[...] if plan.held == KMAX else jnp.concatenate([own_ref[2 * n_row :], came_ref[...]], 0)
        packet_out[...] = jnp.where(sc[period] == 1, one, two)
        row_ref[...], col_ref[...] = split_cells(packet_out[:, 2 * count : 3 * count], line_block(plan), rows, cols)

        def line(i, carry):
            sample_line(grid_ref[i], row_ref, col_ref, real_ref, imag_ref, i, rows, cols, count)
            return carry

        lax.fori_loop(0, lines, line, 0)
        slot = cut * plan.per_cut + me * plan.held + lax.div(lax.broadcasted_iota(jnp.int32, (lines, count), 0), jnp.int32(n_row))
        fresh = remainder(slot - plan.lead + shifted_total(sc, period), plan.slots) < sc[period]
        emit_real, emit_imag = kick(packet_out, real_ref, imag_ref, fresh, period, count)
        emit_out[:lines] = emit_real
        emit_out[lines:] = emit_imag
        if last:
            outs = refs[:n_row]
            for d in range(n_row):
                for h in range(plan.held):
                    line_at = pl.ds(h * n_row + (me ^ d), 1)
                    outs[d][h : h + 1, : 2 * count] = packet_out[line_at, : 2 * count]
                    sums = packet_out[h * n_row : (h + 1) * n_row, 3 * count :]
                    outs[d][h : h + 1, 2 * count :] = jnp.sum(sums, 0, keepdims=True)

    outs = [sds((lines, width)), sds((2 * lines, count))]
    if last:
        outs += [sds((plan.held, 2 * count + LANES))] * n_row
    return vmem_call(kernel, outs, [grid, own, came], shifts, [pltpu.VMEM((lines, count), F32)] * 4)


def deposit_and_sweep(plan, period, grids, packet, emit, props, shifts):
    count, rows, cols, lines, n_row, held = plan.count, plan.rows, plan.cols, plan.lines, plan.n_row, plan.held
    all_rows = n_row * rows
    first, last = period == 0, period + 1 == plan.periods
    n_grids = len(grids)

    def kernel(sc, *refs):
        grid_refs = refs[:n_grids]
        packet_ref, emit_ref, row_high, row_low, col_high, col_low = refs[n_grids : n_grids + 6]
        outs = refs[n_grids + 6 : -7]
        row_ref, col_ref, high_ref, low_ref, mid_high, mid_low, done_ref = refs[-7:]
        me, cut = lax.axis_index("row"), lax.axis_index("cuts")
        row_ref[...], col_ref[...] = split_cells(packet_ref[:, 2 * count : 3 * count], line_block(plan), rows, cols)

        def slot(h, carry):
            index = remainder(cut * plan.per_cut + me * held + h - plan.lead + shifted_total(sc, period), plan.slots)
            keep = jnp.where(index < sc[period], 0.0, 1.0).astype(F32)

            def line(b, piece):
                i = h * n_row + b
                total = jnp.zeros((4 * rows, cols), F32)
                for start, step in chunks(count):
                    span = pl.ds(start, step)
                    pick = one_hot(col_ref[pl.ds(i, 1), span], cols)
                    level = lax.broadcasted_iota(jnp.int32, (rows, step), 0).astype(BF)
                    mask = level == jnp.broadcast_to(row_ref[pl.ds(i, 1), span].astype(BF), (rows, step))
                    weights = []
                    for part in range(2):
                        for half in halves(emit_ref[pl.ds(part * lines + i, 1), span]):
                            weights.append(jnp.where(mask, jnp.broadcast_to(half, (rows, step)), jnp.zeros((), BF)))
                    total += lax.dot_general(
                        jnp.concatenate(weights, 0), pick, (((1,), (1,)), ((), ())), preferred_element_type=F32
                    )
                for part in range(2):
                    base = 2 * part * rows
                    if first:
                        held_value = grid_refs[piece][part, h]
                    else:
                        held_value = grid_refs[0][i, pl.ds(base, rows), :].astype(F32)
                        held_value += grid_refs[0][i, pl.ds(base + rows, rows), :].astype(F32)
                    added = total[base : base + rows] + total[base + rows : base + 2 * rows]
                    high, low = halves(keep * held_value + source_gain * added)
                    where = (pl.ds(pl.multiple_of(b * rows, rows), rows), pl.ds(part * cols, cols))
                    high_ref[where] = high
                    low_ref[where] = low

            if first:
                for d in range(n_row):
                    line(me ^ d, d)
            else:
                def step_line(b, inner):
                    line(b, None)
                    return inner

                lax.fori_loop(0, n_row, step_line, 0)
            high = high_ref[...]
            swept = jnp.dot(high, col_high[...], preferred_element_type=F32)
            swept += jnp.dot(high, col_low[...], preferred_element_type=F32)
            swept += jnp.dot(low_ref[...], col_high[...], preferred_element_type=F32)
            for part in range(2):
                high, low = halves(swept[:, part * cols : (part + 1) * cols])
                mid_high[pl.ds(part * all_rows, all_rows), :] = high
                mid_low[pl.ds(part * all_rows, all_rows), :] = low
            high = mid_high[...]
            result = jnp.dot(row_high[...], high, preferred_element_type=F32)
            result += jnp.dot(row_low[...], high, preferred_element_type=F32)
            result += jnp.dot(row_high[...], mid_low[...], preferred_element_type=F32)
            if last:
                done_ref[...] = result
                for part in range(2):
                    for d in range(n_row):
                        from_row = pl.multiple_of(part * all_rows + (me ^ d) * rows, rows)
                        outs[d][part, h] = done_ref[pl.ds(from_row, rows), :]
            else:
                for part in range(2):
                    for b in range(n_row):
                        high, low = halves(result[part * all_rows + b * rows : part * all_rows + (b + 1) * rows])
                        outs[0][h * n_row + b, pl.ds(2 * part * rows, rows), :] = high
                        outs[0][h * n_row + b, pl.ds((2 * part + 1) * rows, rows), :] = low
            return carry

        lax.fori_loop(0, held, slot, 0)

    if last:
        outs = [sds((2, held, rows, cols))] * n_row
    else:
        outs = [sds((lines, 4 * rows, cols), BF)]
    scratch = [
        pltpu.VMEM((lines, count), F32),
        pltpu.VMEM((lines, count), F32),
        pltpu.VMEM((all_rows, 2 * cols), BF),
        pltpu.VMEM((all_rows, 2 * cols), BF),
        pltpu.VMEM((2 * all_rows, cols), BF),
        pltpu.VMEM((2 * all_rows, cols), BF),
        pltpu.VMEM((2 * all_rows, cols), F32),
    ]
    return vmem_call(kernel, outs, [*grids, packet, emit, *props], shifts, scratch)


def split_props(row_prop, col_prop):
    size, cols = row_prop.shape[1], col_prop.shape[1]

    def kernel(row_ref, col_ref, row_high, row_low, col_high, col_low):
        def put(high_ref, low_ref, top, left, value):
            where = (slice(top, top + value.shape[0]), slice(left, left + value.shape[1]))
            high_ref[where], low_ref[where] = halves(value)

        put(row_high, row_low, 0, 0, row_ref[0])
        put(row_high, row_low, 0, size, -row_ref[1])
        put(row_high, row_low, size, 0, row_ref[1])
        put(row_high, row_low, size, size, row_ref[0])
        real, imag = col_ref[0].T, col_ref[1].T
        put(col_high, col_low, 0, 0, real)
        put(col_high, col_low, 0, cols, imag)
        put(col_high, col_low, cols, 0, -imag)
        put(col_high, col_low, cols, cols, real)

    outs = [sds((2 * size, 2 * size), BF)] * 2 + [sds((2 * cols, 2 * cols), BF)] * 2
    return vmem_call(kernel, outs, [row_prop, col_prop])


def edges(plan, pieces, axis):
    shape = list(pieces[0].shape)
    parts = [(plan.held - plan.ahead, plan.held, plan.n_row - 1), (0, plan.behind, 0)]
    parts = [part for part in parts if part[1] > part[0]]
    outs = [sds(tuple(shape[:axis] + [stop - start] + shape[axis + 1 :])) for start, stop, _ in parts]

    def kernel(*refs):
        me = lax.axis_index("row")
        for d in range(plan.n_row):
            for (start, stop, owner), out in zip(parts, refs[plan.n_row :]):
                @pl.when((me ^ d) == owner)
                def _(d=d, start=start, stop=stop, out=out):
                    span = slice(start, stop)
                    out[...] = refs[d][:, span] if axis else refs[d][span]

    return vmem_call(kernel, outs, pieces)


def slipped(plan, pieces, axis):
    ring = [(c, (c + 1) % plan.n_cuts) for c in range(plan.n_cuts)]
    kept = edges(plan, pieces, axis)
    moved = []
    if plan.ahead:
        moved.append(lax.ppermute(kept[0], "cuts", ring))
    if plan.behind:
        moved.append(lax.ppermute(kept[-1], "cuts", [(b, a) for a, b in ring]))
    return moved


def joined_at(plan, refs, target, put):
    me = lax.axis_index("row")
    extra = refs[plan.n_row :]
    if plan.ahead:
        for h in range(plan.ahead):
            put(h, extra[0], h)
    for d in range(plan.n_row):
        for h in range(plan.held):
            put(plan.ahead + (me ^ d) * plan.held + h, refs[d], h)
    for h in range(plan.behind):
        put(plan.ahead + plan.per_cut + h, extra[-1], h)


def first_index(plan, sc):
    return plan.ahead - (shifted_total(sc, plan.periods - 1) - plan.lead)


def finish_electrons(plan, pieces, moved, shifts):
    count, per_cut = plan.count, plan.per_cut
    many = len(pieces) + len(moved)

    def kernel(sc, *refs):
        phase_out, energy_out, sums_out, all_ref = refs[many:]

        def put(index, ref, h):
            all_ref[pl.ds(index, 1), :] = ref[h : h + 1, :]

        joined_at(plan, refs[:many], all_ref, put)
        start = first_index(plan, sc)
        for j in range(per_cut):
            line = all_ref[pl.ds(start + j, 1), :]
            phase_out[j : j + 1, :] = line[:, :count]
            energy_out[j : j + 1, :] = line[:, count : 2 * count]
            sums_out[j : j + 1, :] = line[:, 2 * count :]

    outs = [sds((per_cut, count)), sds((per_cut, count)), sds((per_cut, LANES))]
    scratch = [pltpu.VMEM((per_cut + plan.ahead + plan.behind, 2 * count + LANES), F32)]
    return vmem_call(kernel, outs, [*pieces, *moved], shifts, scratch)


def finish_field(plan, pieces, moved, shifts):
    parts, _, rows, cols = pieces[0].shape
    many = len(pieces) + len(moved)

    def kernel(sc, *refs):
        out, all_ref = refs[many:]

        def put(index, ref, h):
            for part in range(parts):
                all_ref[part, index] = ref[part, h]

        joined_at(plan, refs[:many], all_ref, put)
        start = first_index(plan, sc)
        for part in range(parts):
            for j in range(plan.per_cut):
                out[part, j] = all_ref[part, start + j]

    scratch = [pltpu.VMEM((parts, plan.per_cut + plan.ahead + plan.behind, rows, cols), F32)]
    return vmem_call(kernel, sds((parts, plan.per_cut, rows, cols)), [*pieces, *moved], shifts, scratch)


def whole_slices(plan, field, row_prop, col_prop, phase, energy, cells, shifts):
    n_cuts, n_row, held, count = plan.n_cuts, plan.n_row, plan.held, plan.count
    me = lax.axis_index("row").astype(jnp.int32)
    both = ("cuts", "row")
    head = jnp.concatenate([phase[:KMAX], energy[:KMAX], cells[:KMAX].astype(F32)], 1)
    came = lax.ppermute(head, "cuts", [((c + 1) % n_cuts, c) for c in range(n_cuts)])
    tables = [plan.spread_table(d) for d in range(n_row)]
    pieces = []
    for d in range(n_row):
        pair = lax.rem((me ^ d) + n_row * plan.turn - plan.turn, n_row)
        pieces.append(lax.ppermute(lax.dynamic_slice_in_dim(field, pair * held, held, 1), both, tables[d]))
    props = split_props(row_prop, col_prop)
    packets = first_kick(plan, field, phase, energy, cells, came, shifts)
    packets = [lax.ppermute(packet, both, table) for packet, table in zip(packets, tables)]
    packet, emit = gather_packet(plan, packets)

    devices = n_cuts * n_row
    back = [(source, (source - 1) % devices) for source in range(devices)]
    rounds = [[(r, r ^ d) for r in range(n_row)] for d in range(n_row)]
    grids = pieces
    for period in range(plan.periods):
        last = period + 1 == plan.periods
        if period:
            packet, emit, *homeward = sample_and_kick(plan, period, grids[0], packet, came, shifts)
        if last:
            homeward = [value if d == 0 else lax.ppermute(value, "row", rounds[d]) for d, value in enumerate(homeward)]
            moved = slipped(plan, homeward, 0)
            phase, energy, sums = finish_electrons(plan, homeward, moved, shifts)
        else:
            came = lax.ppermute(packet[: KMAX * n_row], both, back)
        grids = deposit_and_sweep(plan, period, grids, packet, emit, props, shifts)
    pieces = [value if d == 0 else lax.ppermute(value, "row", rounds[d]) for d, value in enumerate(grids)]
    field = finish_field(plan, pieces, slipped(plan, pieces, 1), shifts)
    bunching = sums[:, : 2 * plan.periods].T.reshape(plan.periods, 2, plan.per_cut) * (count * n_row) ** (-0.5)
    return field, phase, energy, bunching


def solution(mesh):
    n_cuts, n_row = mesh.shape["cuts"], mesh.shape["row"]

    def body(field, row_prop, col_prop, phase, energy, cells, shifts):
        plan = Plan(n_cuts, n_row, field, phase, shifts)
        if plan.fits():
            return whole_slices(plan, field, row_prop, col_prop, phase, energy, cells, shifts)
        return row_blocks(field, row_prop, col_prop, phase, energy, cells, shifts)

    return jax.shard_map(
        body,
        mesh=mesh,
        in_specs=(
            P(None, "cuts", "row", None),
            P(),
            P(),
            P("cuts", "row"),
            P("cuts", "row"),
            P("cuts", "row"),
            P(),
        ),
        out_specs=(
            P(None, "cuts", "row", None),
            P("cuts", "row"),
            P("cuts", "row"),
            P(None, None, "cuts"),
        ),
        check_vma=False,
    )
```

```python
import jax
import jax.numpy as jnp
from jax import lax
from jax.experimental import pallas as pl
from jax.experimental.pallas import tpu as pltpu
from jax.sharding import PartitionSpec as P


KMAX = 2
kick_rate = 0.5
source_gain = 0.5
BF = jnp.bfloat16
F32 = jnp.float32
LANES = 128
CHUNK = 512


def shifted(value, axis, steps):
    count = lax.axis_size(axis)
    initial, last = (max(0, -steps), min(count, count - steps))
    return lax.ppermute(value, axis, [(source, source + steps) for source in range(initial, last)])


def rows_product(matrix, values):
    return jnp.einsum("rk,skc->src", matrix, values, precision=lax.Precision.HIGHEST)


def cols_product(matrix, values):
    return jnp.einsum("ck,srk->src", matrix, values, precision=lax.Precision.HIGHEST)


def complex_rows(prop, values):
    return jnp.stack(
        [
            rows_product(prop[0], values[0]) - rows_product(prop[1], values[1]),
            rows_product(prop[0], values[1]) + rows_product(prop[1], values[0]),
        ]
    )


def row_blocks(field, row_prop, col_prop, phase, energy, cells, shifts):
    count = field.shape[1]
    row_count = field.shape[2]
    col_count = field.shape[3]
    row_start = lax.axis_index("row") * row_count
    local_cells = cells - row_start * col_count
    cell_row = local_cells // col_count
    cell_col = local_cells - cell_row * col_count
    row_pick = (
        cell_row[:, None, :] == jnp.arange(row_count, dtype=jnp.int32)[None, :, None]
    ).astype(jnp.float32)
    col_pick = (
        cell_col[:, :, None] == jnp.arange(col_count, dtype=jnp.int32)[None, None, :]
    ).astype(jnp.float32)
    own_prop = lax.dynamic_slice_in_dim(row_prop, row_start, row_count, 1)
    partials = []
    for period in range(shifts.shape[0]):
        last_slices = field[:, count - KMAX :]
        arrived = shifted(last_slices, "cuts", 1)
        joined = jnp.concatenate([arrived, field], axis=1)
        field = lax.dynamic_slice_in_dim(joined, KMAX - shifts[period], count, 1)
        by_column = jnp.einsum("psrc,sec->psre", field, col_pick, precision=lax.Precision.HIGHEST)
        samples = jnp.sum(by_column * row_pick[None], axis=2)
        sample_real = samples[0]
        sample_imag = samples[1]
        energy = energy - kick_rate * (sample_real * jnp.cos(phase) - sample_imag * jnp.sin(phase))
        phase = phase + energy
        emit_real = jnp.cos(phase)
        emit_imag = -jnp.sin(phase)
        local_sums = jnp.stack([jnp.sum(emit_real, 1), jnp.sum(emit_imag, 1)])
        partials.append(lax.psum(local_sums, "row"))
        emitted = jnp.stack([emit_real, emit_imag])
        weighted = row_pick[None] * emitted[:, :, None, :]
        deposit = jnp.einsum("psre,sec->psrc", weighted, col_pick, precision=lax.Precision.HIGHEST)
        field = field + source_gain * deposit
        field = jnp.stack(
            [
                cols_product(col_prop[0], field[0]) - cols_product(col_prop[1], field[1]),
                cols_product(col_prop[0], field[1]) + cols_product(col_prop[1], field[0]),
            ]
        )
        field = complex_rows(own_prop, lax.all_gather(field, "row", axis=2, tiled=True))
    bunching = jnp.stack(partials)
    bunching = bunching * (phase.shape[1] * lax.axis_size("row")) ** (-0.5)
    return (field, phase, energy, bunching)


def halves(value):
    high = value.astype(BF)
    return high, (value - high.astype(F32)).astype(BF)


def one_hot(index, size):
    shape = (size, index.shape[1])
    level = lax.broadcasted_iota(jnp.int32, shape, 0).astype(BF)
    return jnp.where(level == jnp.broadcast_to(index.astype(BF), shape), jnp.ones((), BF), jnp.zeros((), BF))


def chunks(length):
    step = CHUNK if length % CHUNK == 0 else length
    return [(start, step) for start in range(0, length, step)]


def vmem_call(kernel, outs, inputs, shifts=None, scratch=(), out_specs=None):
    vmem = pl.BlockSpec(memory_space=pltpu.VMEM)
    specs = [vmem] * len(inputs)
    if shifts is not None:
        specs = [pl.BlockSpec(memory_space=pltpu.SMEM)] + specs
        inputs = [shifts] + list(inputs)
    return pl.pallas_call(
        kernel,
        out_shape=outs,
        in_specs=specs,
        out_specs=out_specs or jax.tree.map(lambda _: vmem, outs),
        scratch_shapes=list(scratch),
        compiler_params=pltpu.CompilerParams(vmem_limit_bytes=32 * 1024 * 1024),
    )(*inputs)


def sds(shape, dtype=F32):
    return jax.ShapeDtypeStruct(shape, dtype)


def remainder(value, divisor):
    return lax.rem(value + 4 * divisor, jnp.int32(divisor))


def ring_place(row):
    place, shift = row, 1
    while shift < 16:
        place = place ^ (place >> shift)
        shift *= 2
    return place


def ring_row(place):
    return place ^ (place >> 1)


class Plan:
    def __init__(self, n_cuts, n_row, field, phase, shifts):
        self.n_cuts, self.n_row = n_cuts, n_row
        self.per_cut, self.rows, self.cols = field.shape[1:]
        self.count = phase.shape[1]
        self.periods = shifts.shape[0]
        self.held = max(1, self.per_cut // n_row)
        self.slots = n_cuts * self.per_cut
        self.lines = self.held * n_row
        self.farthest = KMAX * self.periods
        self.line_rows = self.count // self.cols
        self.field_rows = 2 * self.rows
        self.home_rows = self.field_rows + -(-(2 * self.line_rows + 1) // 8) * 8

    def fits(self):
        n = self.n_row
        if n & (n - 1) or self.per_cut % n or self.held < KMAX or self.count % self.cols or self.cols % LANES:
            return False
        return self.farthest <= self.per_cut


def split_cells(cells, block, rows, cols):
    flat = cells.astype(jnp.int32)
    row = lax.div(flat, jnp.int32(cols))
    column = flat - row * cols
    return (row - block * rows).astype(F32), column.astype(F32)


def sample_line(values, row_ref, col_ref, real_ref, imag_ref, i, rows, cols, count):
    for start, step in chunks(count):
        here = (pl.ds(i, 1), pl.ds(start, step))
        found = jnp.dot(values, one_hot(col_ref[here], cols), preferred_element_type=F32)
        mask = lax.broadcasted_iota(jnp.int32, (rows, step), 0).astype(F32) == row_ref[here]
        real = jnp.where(mask, found[:rows] + found[rows : 2 * rows], 0.0)
        imag = jnp.where(mask, found[2 * rows : 3 * rows] + found[3 * rows :], 0.0)
        real_ref[here] = jnp.sum(real, 0, keepdims=True)
        imag_ref[here] = jnp.sum(imag, 0, keepdims=True)


def shifted_total(sc, period):
    total = sc[0]
    for step in range(1, period + 1):
        total = total + sc[step]
    return total


REDUCED_UP_TO = 8192.0


def sine_cosine(angle):
    rounder = 12582912.0
    turns = (angle * 0.6366197723675814 + rounder) - rounder
    rest = angle - turns * 1.5703125
    rest = rest - turns * 4.837512969970703125e-4
    rest = rest - turns * 7.54978995489188216e-8
    square = rest * rest
    sine = rest + rest * square * (-1.6666654611e-1 + square * (8.3321608736e-3 - square * 1.9515295891e-4))
    cosine = 4.166664568298827e-2 + square * (-1.388731625493765e-3 + square * 2.443315711809948e-5)
    cosine = 1.0 - 0.5 * square + square * square * cosine
    quarter = turns.astype(jnp.int32)
    odd = (quarter & 1) == 1
    sine, cosine = jnp.where(odd, cosine, sine), jnp.where(odd, sine, cosine)
    sine = jnp.where((quarter & 2) == 2, -sine, sine)
    return sine, jnp.where(((quarter + 1) & 2) == 2, -cosine, cosine)


def put_sine_cosine(angle, sine_ref, cosine_ref):
    sine_ref[...], cosine_ref[...] = sine_cosine(angle)

    @pl.when(jnp.logical_not(jnp.max(jnp.abs(angle)) <= REDUCED_UP_TO))
    def _():
        sine_ref[...] = jnp.sin(angle)
        cosine_ref[...] = jnp.cos(angle)


def kick(packet_ref, real_ref, imag_ref, sine_ref, cosine_ref, fresh, period, count):
    phase = packet_ref[:, :count]
    put_sine_cosine(phase, sine_ref, cosine_ref)
    change = kick_rate * (real_ref[...] * cosine_ref[...] - imag_ref[...] * sine_ref[...])
    energy = packet_ref[:, count : 2 * count] - jnp.where(fresh, 0.0, change)
    phase = phase + energy
    packet_ref[:, :count] = phase
    packet_ref[:, count : 2 * count] = energy
    put_sine_cosine(phase, sine_ref, cosine_ref)
    sums = packet_ref[:, 3 * count :]
    lane = lax.broadcasted_iota(jnp.int32, sums.shape, 1)
    sums = jnp.where(lane == 2 * period, jnp.sum(cosine_ref[...], 1, keepdims=True), sums)
    sums = jnp.where(lane == 2 * period + 1, -jnp.sum(sine_ref[...], 1, keepdims=True), sums)
    packet_ref[:, 3 * count :] = sums


def first_kick(plan, field, phase, energy, cells, came, shifts):
    count, rows, cols, lines = plan.count, plan.rows, plan.cols, plan.per_cut

    def kernel(sc, field_ref, phase_ref, energy_ref, cells_ref, came_ref, *refs):
        outs = refs[: plan.n_row]
        total_out, packet_ref, row_ref, col_ref, real_ref, imag_ref, sine_ref, cosine_ref = refs[plan.n_row :]
        total_out[0] = shifted_total(sc, plan.periods - 1)
        me, cut = lax.axis_index("row"), lax.axis_index("cuts")
        parts = (phase_ref[...], energy_ref[...], cells_ref[...].astype(F32))
        for place, part in enumerate(parts):
            span = slice(place * count, (place + 1) * count)
            one = jnp.concatenate([part[1:], came_ref[:1, span]], 0)
            two = jnp.concatenate([part[2:], came_ref[:2, span]], 0)
            packet_ref[:, span] = jnp.where(sc[0] == 1, one, two)
        packet_ref[:, 3 * count :] = jnp.zeros((lines, LANES), F32)
        row_ref[...], col_ref[...] = split_cells(packet_ref[:, 2 * count : 3 * count], me, rows, cols)

        def line(i, carry):
            values = jnp.concatenate([*halves(field_ref[0, i]), *halves(field_ref[1, i])], 0)
            sample_line(values, row_ref, col_ref, real_ref, imag_ref, i, rows, cols, count)
            return carry

        lax.fori_loop(0, lines, line, 0, unroll=4)
        place = cut * plan.per_cut + lax.broadcasted_iota(jnp.int32, (lines, count), 0)
        kick(packet_ref, real_ref, imag_ref, sine_ref, cosine_ref, remainder(place + sc[0], plan.slots) < sc[0], 0, count)
        for d in range(plan.n_row):
            for h in range(plan.held):
                outs[d][h : h + 1, :] = packet_ref[pl.ds(ring_place(me ^ d) * plan.held + h, 1), :]

    width = 3 * count + LANES
    scratch = [pltpu.VMEM((lines, width), F32)] + [pltpu.VMEM((lines, count), F32)] * 6
    outs = [sds((plan.held, width))] * plan.n_row + [sds((1,), jnp.int32)]
    vmem = pl.BlockSpec(memory_space=pltpu.VMEM)
    smem = pl.BlockSpec(memory_space=pltpu.SMEM)
    return vmem_call(kernel, outs, [field, phase, energy, cells, came], shifts, scratch, [vmem] * plan.n_row + [smem])


def gather_packet(plan, pieces):
    count, lines = plan.count, plan.lines

    def kernel(*refs):
        packet_out, cosine_out, sine_out = refs[plan.n_row :]
        me = lax.axis_index("row")
        for d in range(plan.n_row):
            for h in range(plan.held):
                packet_out[pl.ds(h * plan.n_row + (me ^ d), 1), :] = refs[d][h : h + 1, :]
        put_sine_cosine(packet_out[:, :count], sine_out, cosine_out)

    return vmem_call(kernel, (sds((lines, 3 * count + LANES)), sds((lines, count)), sds((lines, count))), list(pieces))


def line_block(plan):
    return lax.rem(lax.broadcasted_iota(jnp.int32, (plan.lines, plan.count), 0), jnp.int32(plan.n_row))


def sample_and_kick(plan, period, grid, own, came, shifts):
    count, rows, cols, lines, n_row = plan.count, plan.rows, plan.cols, plan.lines, plan.n_row
    width = 3 * count + LANES

    def kernel(sc, grid_ref, own_ref, came_ref, packet_out, cosine_out, sine_out, *refs):
        row_ref, col_ref, real_ref, imag_ref = refs[-4:]
        me, cut = lax.axis_index("row"), lax.axis_index("cuts")
        one = jnp.concatenate([own_ref[n_row:], came_ref[:n_row]], 0)
        two = came_ref[...] if plan.held == KMAX else jnp.concatenate([own_ref[2 * n_row :], came_ref[...]], 0)
        packet_out[...] = jnp.where(sc[period] == 1, one, two)
        row_ref[...], col_ref[...] = split_cells(packet_out[:, 2 * count : 3 * count], line_block(plan), rows, cols)

        def line(i, carry):
            sample_line(grid_ref[i], row_ref, col_ref, real_ref, imag_ref, i, rows, cols, count)
            return carry

        lax.fori_loop(0, lines, line, 0, unroll=4)
        slot = cut * plan.per_cut + ring_place(me) * plan.held + lax.div(lax.broadcasted_iota(jnp.int32, (lines, count), 0), jnp.int32(n_row))
        fresh = remainder(slot + shifted_total(sc, period), plan.slots) < sc[period]
        kick(packet_out, real_ref, imag_ref, sine_out, cosine_out, fresh, period, count)

    outs = [sds((lines, width)), sds((lines, count)), sds((lines, count))]
    return vmem_call(kernel, outs, [grid, own, came], shifts, [pltpu.VMEM((lines, count), F32)] * 4)


def deposit_and_sweep(plan, period, grids, packet, emit, props, shifts):
    count, rows, cols, lines, n_row, held = plan.count, plan.rows, plan.cols, plan.lines, plan.n_row, plan.held
    all_rows = n_row * rows
    first, last = period == 0, period + 1 == plan.periods
    n_grids = len(grids)

    def kernel(sc, *refs):
        grid_refs = refs[:n_grids]
        packet_ref, cosine_ref, sine_ref, row_both, col_high, col_low = refs[n_grids : n_grids + 6]
        outs = refs[n_grids + 6 : -6]
        row_ref, col_ref, halves_ref, mid_high, mid_low, done_ref = refs[-6:]
        me, cut = lax.axis_index("row"), lax.axis_index("cuts")
        row_ref[...], col_ref[...] = split_cells(packet_ref[:, 2 * count : 3 * count], line_block(plan), rows, cols)
        low_from = held * all_rows

        def line(h, b, piece):
            i = h * n_row + b
            index = remainder(cut * plan.per_cut + ring_place(me) * held + h + shifted_total(sc, period), plan.slots)
            keep = jnp.where(index < sc[period], 0.0, 1.0).astype(F32)
            total = jnp.zeros((4 * rows, cols), F32)
            for start, step in chunks(count):
                span = pl.ds(start, step)
                pick = one_hot(col_ref[pl.ds(i, 1), span], cols)
                level = lax.broadcasted_iota(jnp.int32, (rows, step), 0).astype(BF)
                mask = level == jnp.broadcast_to(row_ref[pl.ds(i, 1), span].astype(BF), (rows, step))
                weights = []
                for value in (cosine_ref[pl.ds(i, 1), span], -sine_ref[pl.ds(i, 1), span]):
                    for half in halves(source_gain * value):
                        weights.append(jnp.where(mask, jnp.broadcast_to(half, (rows, step)), jnp.zeros((), BF)))
                total += lax.dot_general(
                    jnp.concatenate(weights, 0), pick, (((1,), (1,)), ((), ())), preferred_element_type=F32
                )
            for part in range(2):
                base = 2 * part * rows
                if first:
                    held_value = grid_refs[piece][part, h]
                else:
                    held_value = grid_refs[0][i, pl.ds(base, rows), :].astype(F32)
                    held_value += grid_refs[0][i, pl.ds(base + rows, rows), :].astype(F32)
                added = total[base : base + rows] + total[base + rows : base + 2 * rows]
                high, low = halves(keep * held_value + added)
                at = pl.multiple_of(h * all_rows + b * rows, rows)
                halves_ref[pl.ds(at, rows), pl.ds(part * cols, cols)] = high
                halves_ref[pl.ds(low_from + at, rows), pl.ds(part * cols, cols)] = low

        def slot_lines(h, carry):
            for d in range(n_row):
                line(h, me ^ d if first else d, d)
            return carry

        lax.fori_loop(0, held, slot_lines, 0)
        for part in range(2):
            span = slice(part * cols, (part + 1) * cols)
            swept = jnp.dot(halves_ref[...], col_high[:, span], preferred_element_type=F32)
            rest = jnp.dot(halves_ref[:low_from], col_low[:, span], preferred_element_type=F32)
            high, low = halves(swept[:low_from] + swept[low_from:] + rest)
            for h in range(held):
                mid_high[h, part * all_rows : (part + 1) * all_rows] = high[h * all_rows : (h + 1) * all_rows]
                mid_low[h, part * all_rows : (part + 1) * all_rows] = low[h * all_rows : (h + 1) * all_rows]
        both = 2 * all_rows
        for h in range(held):
            swept = jnp.dot(row_both[...], mid_high[h], preferred_element_type=F32)
            result = swept[:both] + swept[both:] + jnp.dot(row_both[:both], mid_low[h], preferred_element_type=F32)
            if last:
                done_ref[...] = result
                for part in range(2):
                    for d in range(n_row):
                        from_row = pl.multiple_of(part * all_rows + (me ^ d) * rows, rows)
                        outs[d][h, part * rows : (part + 1) * rows, :] = done_ref[pl.ds(from_row, rows), :]
            else:
                for part in range(2):
                    for b in range(n_row):
                        high, low = halves(result[part * all_rows + b * rows : part * all_rows + (b + 1) * rows])
                        outs[0][h * n_row + b, 2 * part * rows : (2 * part + 1) * rows, :] = high
                        outs[0][h * n_row + b, (2 * part + 1) * rows : (2 * part + 2) * rows, :] = low

        if last:
            per_line = plan.line_rows
            for h in range(held):
                for d in range(n_row):
                    out = outs[d].at[h]
                    for which in range(2):
                        for t in range(per_line):
                            at = plan.field_rows + which * per_line + t
                            from_col = which * count + t * cols
                            value = packet_ref[pl.ds(h * n_row + (me ^ d), 1), from_col : from_col + cols]
                            out[at : at + 1, :] = value
                    at = plan.field_rows + 2 * per_line
                    out[at:, :] = jnp.zeros((plan.home_rows - at, cols), F32)
                    sums = packet_ref[h * n_row : (h + 1) * n_row, 3 * count :]
                    out[at : at + 1, :LANES] = jnp.sum(sums, 0, keepdims=True)

    if last:
        outs = [sds((held, plan.home_rows, cols))] * n_row
    else:
        outs = [sds((lines, 4 * rows, cols), BF)]
    scratch = [
        pltpu.VMEM((lines, count), F32),
        pltpu.VMEM((lines, count), F32),
        pltpu.VMEM((2 * held * all_rows, 2 * cols), BF),
        pltpu.VMEM((held, 2 * all_rows, cols), BF),
        pltpu.VMEM((held, 2 * all_rows, cols), BF),
        pltpu.VMEM((2 * all_rows, cols), F32),
    ]
    return vmem_call(kernel, outs, [*grids, packet, *emit, *props], shifts, scratch)


def split_props(row_prop, col_prop):
    size, cols = row_prop.shape[1], col_prop.shape[1]

    def kernel(row_ref, col_ref, row_both, col_high, col_low):
        for top, left, value in (
            (0, 0, row_ref[0]), (0, size, -row_ref[1]), (size, 0, row_ref[1]), (size, size, row_ref[0])
        ):
            high, low = halves(value)
            row_both[top : top + size, left : left + size] = high
            row_both[2 * size + top : 2 * size + top + size, left : left + size] = low
        real, imag = col_ref[0].T, col_ref[1].T
        for top, left, value in ((0, 0, real), (0, cols, imag), (cols, 0, -imag), (cols, cols, real)):
            where = (slice(top, top + cols), slice(left, left + cols))
            col_high[where], col_low[where] = halves(value)

    outs = [sds((4 * size, 2 * size), BF)] + [sds((2 * cols, 2 * cols), BF)] * 2
    return vmem_call(kernel, outs, [row_prop, col_prop])


def finish(plan, total, pieces):
    n_row, per_cut, held, rows, cols = plan.n_row, plan.per_cut, plan.held, plan.rows, plan.cols
    count, per_line, periods = plan.count, plan.line_rows, plan.periods
    many = len(pieces)
    at_once = plan.lines // many

    def kernel(*refs):
        field_out, phase_out, energy_out, bunching_out, sums_ref, out_sem = refs[many:]
        me = lax.axis_index("row")
        leaving = []
        places = []
        for at in range(plan.lines):
            d, h = at // held, at % held
            source = refs[at // at_once].at[at % at_once]
            target = lax.rem(ring_place(me ^ d) * held + h + total, jnp.int32(per_cut))
            places.append((source, target))
            for part in range(2):
                part_rows = source.at[pl.ds(part * rows, rows)]
                leaving.append(pltpu.make_async_copy(part_rows, field_out.at[part, target], out_sem.at[at, part]))
                leaving[-1].start()
        for source, target in places:
            for which, out in enumerate((phase_out, energy_out)):
                for t in range(per_line):
                    row = plan.field_rows + which * per_line + t
                    out[pl.ds(target, 1), t * cols : (t + 1) * cols] = source[row : row + 1, :]
            row = plan.field_rows + 2 * per_line
            sums_ref[pl.ds(target, 1), :] = source[row : row + 1, :LANES]
        turned = sums_ref[...].T * (count * n_row) ** (-0.5)
        for period in range(periods):
            bunching_out[period] = turned[2 * period : 2 * period + 2, :]
        for copy in leaving:
            copy.wait()

    outs = [
        sds((2, per_cut, rows, cols)),
        sds((per_cut, count)),
        sds((per_cut, count)),
        sds((periods, 2, per_cut)),
    ]
    vmem, anywhere = pl.BlockSpec(memory_space=pltpu.VMEM), pl.BlockSpec(memory_space=pl.ANY)
    return pl.pallas_call(
        kernel,
        out_shape=outs,
        in_specs=[vmem] * many,
        out_specs=[anywhere] + [vmem] * 3,
        scratch_shapes=[
            pltpu.VMEM((per_cut, LANES), F32),
            pltpu.SemaphoreType.DMA((plan.lines, 2)),
        ],
        compiler_params=pltpu.CompilerParams(vmem_limit_bytes=8 * 1024 * 1024),
    )(*pieces)


def whole_slices(plan, field, row_prop, col_prop, phase, energy, cells, shifts):
    n_cuts, n_row, held = plan.n_cuts, plan.n_row, plan.held
    me = lax.axis_index("row").astype(jnp.int32)
    both = ("cuts", "row")
    head = jnp.concatenate([phase[:KMAX], energy[:KMAX], cells[:KMAX].astype(F32)], 1)
    came = lax.ppermute(head, "cuts", [((c + 1) % n_cuts, c) for c in range(n_cuts)])
    rounds = [[(r, r ^ d) for r in range(n_row)] for d in range(n_row)]

    def to_row(value, d):
        return value if d == 0 else lax.ppermute(value, "row", rounds[d])

    pieces = [to_row(lax.dynamic_slice_in_dim(field, ring_place(me ^ d) * held, held, 1), d) for d in range(n_row)]
    props = split_props(row_prop, col_prop)
    *packets, total = first_kick(plan, field, phase, energy, cells, came, shifts)
    packets = [to_row(packet, d) for d, packet in enumerate(packets)]
    packet, *emit = gather_packet(plan, packets)

    ring = [c * n_row + ring_row(m) for c in range(n_cuts) for m in range(n_row)]
    back = [(device, ring[at - 1]) for at, device in enumerate(ring)]
    grids = pieces
    for period in range(plan.periods):
        if period:
            packet, cosine, sine = sample_and_kick(plan, period, grids[0], packet, came, shifts)
            emit = (cosine, sine)
        if period + 1 < plan.periods:
            came = lax.ppermute(packet[: KMAX * n_row], both, back)
        grids = deposit_and_sweep(plan, period, grids, packet, emit, props, shifts)

    def homeward(steps):
        together = steps % held == 0

        def table(d, h):
            pairs = []
            for c in range(n_cuts):
                for r in range(n_row):
                    cut = (c + (ring_place(r) * held + h + steps) // plan.per_cut) % n_cuts
                    pairs.append((c * n_row + r, cut * n_row + (r ^ d)))
            return pairs

        def send(*values):
            pieces = []
            for d, value in enumerate(values):
                if together:
                    pieces.append(lax.ppermute(value, both, table(d, 0)))
                else:
                    pieces += [lax.ppermute(value[h : h + 1], both, table(d, h)) for h in range(held)]
            return tuple(finish(plan, steps, pieces))

        return send

    totals = range(plan.periods - 1 + KMAX, KMAX * plan.periods + 1)
    branch = jnp.clip(total[0] - totals[0], 0, len(totals) - 1)
    return lax.switch(branch, [homeward(steps) for steps in totals], *grids)


def solution(mesh):
    n_cuts, n_row = mesh.shape["cuts"], mesh.shape["row"]

    def body(field, row_prop, col_prop, phase, energy, cells, shifts):
        plan = Plan(n_cuts, n_row, field, phase, shifts)
        if plan.fits():
            return whole_slices(plan, field, row_prop, col_prop, phase, energy, cells, shifts)
        return row_blocks(field, row_prop, col_prop, phase, energy, cells, shifts)

    return jax.shard_map(
        body,
        mesh=mesh,
        in_specs=(
            P(None, "cuts", "row", None),
            P(),
            P(),
            P("cuts", "row"),
            P("cuts", "row"),
            P("cuts", "row"),
            P(),
        ),
        out_specs=(
            P(None, "cuts", "row", None),
            P("cuts", "row"),
            P("cuts", "row"),
            P(None, None, "cuts"),
        ),
        check_vma=False,
    )
```
